32 devices in a mesh: runs: 2 (over y), amp: 16 (over z, x, core).
Axes of the slice: x: 2, y: 2, z: 4, core: 2. Of those that a mesh axis runs over, the one named last changes fastest.
Arguments:
- initial_state: float32 [256, 128, 128], P(('runs', 'amp')), parts along dimension 0, may hold values from -100 to 100
- gate_angles: float32 [10, 16], P('runs'), parts along dimension 0, may hold values from -3.140625 to 3.140625
- gate_pairs: int32 [5, 16, 2], replicated, may hold values from 0 to 6, as said below
- hop_coef: float32 [23], replicated, may hold values from 0.1 to 0.4
- hop_mask: int32 [23], replicated, may hold values 0 or 1
Outputs:
- adjoint: float32 [256, 128, 128], P(('runs', 'amp')), parts along dimension 0
- block_grads: float32 [10, 128, 128], P('runs'), parts along dimension 0
The draws below stay inside these ranges and needn't reach their ends.
There are 2 independent parts, one for each index of `runs`. The reference program is written for one: setup_inputs(seed, part) draws one part's arguments, and reference() takes and returns one part's arrays. A program takes and returns all parts, laid end to end along the dimension named above; an argument that names none is the same for every part. Nothing has to cross between parts.
Inputs may be any that keep to these rules, and one draw needn't show every extreme that they name: `gate_pairs`: the two qubits of each rotation differ.
All inputs are finite; a program needn't handle non-finite values.
Results may differ from the reference program's by a relative error of at most 0.0003.
Values sent between devices are 32-bit elements; how exact they have to be, the bound alone decides.
A program may use at most 192 MiB of HBM per device.

```python
import math
import jax
import jax.numpy as jnp
from jax import lax

BQ = 7
TQ = 7
YQ = 3
GIV = 16
BS = 128
TOP = 128
CW = 128
BLOCKS = 5
HOPS = 23


def draw_initial_state(key, part):
    row_key, col_key, noise_key = jax.random.split(jax.random.fold_in(key, 11), 3)
    top_ramp = jnp.arange(TOP, dtype=jnp.float32)[:, None, None] / TOP
    mid_ramp = jnp.arange(CW, dtype=jnp.float32)[None, :, None] / CW
    row_scale = jnp.exp(jax.random.uniform(row_key, (TOP, 1, 1), minval=-1.15, maxval=1.15) + 0.55 * top_ramp - 0.3)
    col_scale = jnp.exp(jax.random.uniform(col_key, (1, CW, 1), minval=-1.15, maxval=1.15) + 0.55 * mid_ramp - 0.3)
    noise_part = jax.random.truncated_normal(noise_key, -6.0, 6.0, (TOP, CW, BS))
    return (row_scale * col_scale * noise_part).astype(jnp.float32)


def draw_gate_pairs(key, part):
    first_key, step_key = jax.random.split(jax.random.fold_in(key, 23))
    first_qubit = jax.random.randint(first_key, (BLOCKS, GIV), 0, BQ)
    step_size = jax.random.randint(step_key, (BLOCKS, GIV), 1, BQ)
    second_qubit = (first_qubit + step_size) % BQ
    return jnp.stack([first_qubit, second_qubit], axis=-1).astype(jnp.int32)


def touch_ends(values, rng, least, largest):
    extent = values.shape
    index_at = [jax.random.randint(jax.random.fold_in(rng, axis), (), 0, extent[axis]) for axis in range(len(extent))]
    values = values.at[tuple(index_at)].set(least)
    longest = extent.index(max(extent))
    index_at[longest] = (index_at[longest] + 1) % extent[longest]
    return values.at[tuple(index_at)].set(largest)


def setup_inputs(seed: int = 0, part: int = 0) -> dict:
    key_of = jax.random.split(jax.random.key(seed), 6)
    own_keys = jax.random.split(jax.random.fold_in(key_of[5], part), 6)
    initial_state = draw_initial_state(jax.random.fold_in(jax.random.fold_in(key_of[5], part), 71), part)
    gate_angles = jnp.clip(jax.random.uniform(own_keys[1], (BLOCKS, GIV), jnp.float32, -3.140625, 3.140625), -3.140625, 3.140625)
    gate_pairs = draw_gate_pairs(jax.random.fold_in(key_of[5], 71), part)
    hop_coef = jnp.clip(jnp.exp(jax.random.uniform(key_of[3], (HOPS,), jnp.float32, math.log(0.1), math.log(0.4))), 0.1, 0.4)
    hop_mask = touch_ends((jax.random.randint(key_of[4], (HOPS,), 0, 4) < 3).astype(jnp.int32), jax.random.fold_in(key_of[4], 1), 0, 1)
    return {"initial_state": initial_state, "gate_angles": gate_angles, "gate_pairs": gate_pairs, "hop_coef": hop_coef, "hop_mask": hop_mask}


exact_mode = lax.Precision.HIGHEST


def build_block(angles, pair_list, block_size):
    positions = jnp.arange(block_size, dtype=jnp.int32)
    diagonal = positions[:, None] == positions[None, :]

    def rotate(product, element):
        angle_now, pair_now = element
        one_bit = jnp.right_shift(positions, pair_now[0]) & 1
        two_bit = jnp.right_shift(positions, pair_now[1]) & 1
        flip_mask = jnp.left_shift(jnp.int32(1), pair_now[0]) | jnp.left_shift(jnp.int32(1), pair_now[1])
        partner = jnp.bitwise_xor(positions, flip_mask)
        differ = (one_bit != two_bit)[:, None]
        zero_value = jnp.zeros((), product.dtype)
        one_value = jnp.ones((), product.dtype)
        sine_value = jnp.sin(angle_now)
        signed = jnp.where(one_bit < two_bit, -sine_value, sine_value)[:, None]
        rotation = jnp.where(diagonal, jnp.where(differ, jnp.cos(angle_now), one_value), zero_value)
        rotation = rotation + jnp.where(differ & (positions[None, :] == partner[:, None]), signed, zero_value)
        return jnp.dot(rotation, product, precision=exact_mode), None

    identity = jnp.eye(block_size, dtype=angles.dtype)
    product, unused = lax.scan(rotate, identity, (angles, pair_list))
    return product


def shaped_for(amplitudes, window):
    top_rows, mid_count, lane_count = amplitudes.shape
    if window == 0:
        return amplitudes
    if window == 1:
        return amplitudes.reshape(top_rows, mid_count // 4, lane_count, 4)
    if window == 2:
        stride = min(2 ** (YQ - 1), mid_count // lane_count)
        return amplitudes.reshape(top_rows, mid_count // (stride * lane_count), lane_count, stride, lane_count)
    if window == 3:
        low_count = 2 ** YQ
        spread = lane_count // low_count
        return amplitudes.reshape(top_rows // spread, spread, mid_count // low_count, low_count, lane_count)
    return amplitudes.reshape(top_rows // lane_count, lane_count, mid_count, lane_count)


def apply_window(amplitudes, unitary, window):
    shaped = shaped_for(amplitudes, window)
    lane_count = amplitudes.shape[2]
    if window == 0:
        result = jnp.einsum('ij,tcj->tci', unitary, shaped, precision=exact_mode)
    elif window == 1:
        result = jnp.einsum('ij,tcja->tcia', unitary, shaped, precision=exact_mode)
    elif window == 2:
        result = jnp.einsum('ij,abjcd->abicd', unitary, shaped, precision=exact_mode)
    elif window == 3:
        low_count = 2 ** YQ
        spread = lane_count // low_count
        folded = unitary.reshape(spread, low_count, spread, low_count)
        result = jnp.einsum('pqkl,akblr->apbqr', folded, shaped, precision=exact_mode)
    else:
        result = jnp.einsum('ij,ajcr->aicr', unitary, shaped, precision=exact_mode)
    return result.reshape(amplitudes.shape)


def window_gram(adjoint, previous, window):
    lane_count = adjoint.shape[2]
    left_side = shaped_for(adjoint, window)
    right_side = shaped_for(previous, window)
    if window == 0:
        result = jnp.einsum('tci,tcj->ij', left_side, right_side, precision=exact_mode)
    elif window == 1:
        result = jnp.einsum('tcia,tcja->ij', left_side, right_side, precision=exact_mode)
    elif window == 2:
        result = jnp.einsum('abicd,abjcd->ij', left_side, right_side, precision=exact_mode)
    elif window == 3:
        result = jnp.einsum('apbqr,akblr->pqkl', left_side, right_side, precision=exact_mode)
    else:
        result = jnp.einsum('aicr,ajcr->ij', left_side, right_side, precision=exact_mode)
    return result.reshape(lane_count, lane_count)


def hop_pair(amplitudes, low_bit, high_bit):
    flat_values = amplitudes.reshape(-1)
    total_size = flat_values.shape[0]
    shaped = flat_values.reshape(total_size // 2 ** (high_bit + 1), 2, 2 ** (high_bit - low_bit - 1), 2, 2 ** low_bit)
    crossed = jnp.transpose(shaped, (0, 3, 2, 1, 4))
    differ = (1.0 - jnp.eye(2, dtype=amplitudes.dtype)).reshape(1, 2, 1, 2, 1)
    return (crossed * differ).reshape(amplitudes.shape)


def hamiltonian(amplitudes, weights):
    mid_count = amplitudes.shape[1]
    middle_bits = mid_count.bit_length() - 1
    first_top = BQ + middle_bits
    hop_pairs = [(position, position + 1) for position in range(BQ + YQ)]
    hop_pairs = hop_pairs + [(first_top + offset, first_top + offset + 1) for offset in range(TQ - 1)]
    hop_pairs = hop_pairs + [(BQ + offset, first_top + offset) for offset in range(TQ)]
    summed = jnp.zeros_like(amplitudes)
    for number in range(len(hop_pairs)):
        low_bit, high_bit = hop_pairs[number]
        summed = summed + weights[number] * hop_pair(amplitudes, low_bit, high_bit)
    return summed


def reference(initial_state, gate_angles, gate_pairs, hop_coef, hop_mask):
    lane_count = initial_state.shape[2]
    weights = hop_coef * hop_mask.astype(hop_coef.dtype)
    gate_blocks = [build_block(gate_angles[number], gate_pairs[number], lane_count) for number in range(BLOCKS)]
    current = initial_state
    for number in range(BLOCKS):
        current = apply_window(current, gate_blocks[number], number % 5)
    adjoint = hamiltonian(current, weights)
    factor = 2.0 / (initial_state.shape[0] * initial_state.shape[1])
    collected = []
    for number in range(BLOCKS - 1, BLOCKS - 6, -1):
        window = number % 5
        transposed = gate_blocks[number].T
        current = apply_window(current, transposed, window)
        collected.append(factor * window_gram(adjoint, current, window))
        adjoint = apply_window(adjoint, transposed, window)
    block_grads = jnp.stack(collected[::-1])
    return adjoint, block_grads
```

```python
import functools
import jax
import jax.numpy as jnp
from jax import lax
from jax.experimental import pallas as pl
from jax.experimental.pallas import tpu as pltpu
from jax.sharding import PartitionSpec as P

YQ = 3
AXIS = "amp"
f32 = jnp.float32
bf16 = jnp.bfloat16
NN = ((1,), (0,))
NT = ((1,), (1,))
TN = ((0,), (0,))


def split(x):
    high = x.astype(bf16)
    return high, (x - high.astype(f32)).astype(bf16)


def dot_of(a, b, dims):
    return lax.dot_general(a, b, (dims, ((), ())), preferred_element_type=f32)


def dot3(a, b, dims=NN):
    ah, al = a if isinstance(a, tuple) else split(a)
    bh, bl = b if isinstance(b, tuple) else split(b)
    return dot_of(ah, bh, dims) + (dot_of(ah, bl, dims) + dot_of(al, bh, dims))


def rows_of(ref, start, size, stride):
    if stride == 1:
        return ref[pl.ds(start, size), :]
    return ref[pl.ds(start, size, stride=stride), :]


def put_rows(ref, start, size, stride, value):
    if stride == 1:
        ref[pl.ds(start, size), :] = value
    else:
        ref[pl.ds(start, size, stride=stride), :] = value


def apply_rows(dst, src, matrix, starts, size, stride):
    halves = split(matrix)
    for start in starts:
        put_rows(dst, start, size, stride, dot3(halves, rows_of(src, start, size, stride)))


def gram_rows(left, right, starts, size, stride, right_stride=None, right_starts=None):
    right_starts = starts if right_starts is None else right_starts
    right_stride = stride if right_stride is None else right_stride
    total = None
    for number in range(0, len(starts), 2):
        pick = range(number, min(number + 2, len(starts)))
        a = jnp.concatenate([rows_of(left, starts[i], size, stride) for i in pick], axis=1)
        b = jnp.concatenate(
            [rows_of(right, right_starts[i], size, right_stride) for i in pick], axis=1
        )
        part = dot3(a, b, NT)
        total = part if total is None else total + part
    return total


def apply_lanes(dst, src, matrix):
    rows = src.shape[0]
    halves = split(matrix)
    step = min(256, rows)
    for start in range(0, rows, step):
        dst[pl.ds(start, step), :] = dot3(src[pl.ds(start, step), :], halves)


def gram_lanes(left, right):
    rows = left.shape[0]
    total = None
    step = min(256, rows)
    for start in range(0, rows, step):
        part = dot3(left[pl.ds(start, step), :], right[pl.ds(start, step), :], TN)
        total = part if total is None else total + part
    return total


def spread_matrix(lanes):
    row = lax.broadcasted_iota(jnp.int32, (4 * lanes, lanes), 0)
    col = lax.broadcasted_iota(jnp.int32, (4 * lanes, lanes), 1)
    return jnp.where(lax.shift_right_logical(row, 2) == col, 1.0, 0.0).astype(bf16)


def same_low(lanes):
    row = lax.broadcasted_iota(jnp.int32, (4 * lanes, 4 * lanes), 0)
    col = lax.broadcasted_iota(jnp.int32, (4 * lanes, 4 * lanes), 1)
    return (row & 3) == (col & 3)


def widen(matrix):
    lanes = matrix.shape[0]
    spread = spread_matrix(lanes)
    keep = same_low(lanes)
    made = []
    for part in split(matrix):
        left = dot_of(spread, part, NN).astype(bf16)
        full = dot_of(left, spread, NT)
        made.append(jnp.where(keep, full, 0.0).astype(bf16))
    return tuple(made)


def quads(ref):
    count = ref.shape[0] // 4
    return jnp.concatenate([ref[pl.ds(q, count, stride=4), :] for q in range(4)], axis=1)


def apply_quads(dst, values, matrix):
    lanes = matrix.shape[0]
    result = dot3(values, widen(matrix))
    count = result.shape[0]
    for q in range(4):
        dst[pl.ds(q, count, stride=4), :] = result[:, q * lanes : (q + 1) * lanes]


def gram_quads(left, right):
    lanes = left[0].shape[1] // 4
    full = jnp.where(same_low(lanes), dot3(left, right, TN), 0.0)
    spread = spread_matrix(lanes)
    fh, fl = split(full)
    half = dot_of(fh, spread, NN) + dot_of(fl, spread, NN)
    hh, hl = split(half)
    return dot_of(spread, hh, TN) + dot_of(spread, hl, TN)


def mid_starts(rows, mid_count, lanes):
    stride = min(2 ** (YQ - 1), mid_count // lanes)
    groups = rows // (stride * lanes)
    return [g * stride * lanes + s for g in range(groups) for s in range(stride)], stride


def front_kernel(mid_count, pairs, x, angles, ut, u, s1, s2, s3):
    blocks, lanes = ut.shape[0], ut.shape[1]
    givens = angles.shape[1]
    cosines = jnp.cos(angles[...])
    sines = jnp.sin(angles[...])
    lane = lax.broadcasted_iota(jnp.int32, (8, lanes), 1)
    row = lax.broadcasted_iota(jnp.int32, (lanes, lanes), 0)
    col = lax.broadcasted_iota(jnp.int32, (lanes, lanes), 1)
    for b in range(blocks):
        ut[b] = jnp.where(row == col, 1.0, 0.0)
    for g in range(givens):
        for b in range(blocks):
            p = pairs[b, g, 0]
            s = pairs[b, g, 1]
            low = lax.shift_right_logical(lane, p) & 1
            high = lax.shift_right_logical(lane, s) & 1
            cosine = jnp.broadcast_to(cosines[b : b + 1, g : g + 1], (8, lanes))
            sine = jnp.broadcast_to(sines[b : b + 1, g : g + 1], (8, lanes))
            keep = jnp.where(low != high, cosine, 1.0)[:1]
            up = jnp.where(low < high, -sine, 0.0)[:1]
            down = jnp.where(low > high, sine, 0.0)[:1]
            gap = lax.shift_left(jnp.int32(1), p) - lax.shift_left(jnp.int32(1), s)
            now = ut[b]
            ut[b] = (
                now * keep
                + pltpu.roll(now, (lanes - gap) & (lanes - 1), 1) * up
                + pltpu.roll(now, (lanes + gap) & (lanes - 1), 1) * down
            )
    for b in range(blocks):
        u[b] = jnp.transpose(ut[b])
    apply_lanes(s1, x, ut[0])
    apply_quads(s2, quads(s1), ut[1])
    starts, stride = mid_starts(x.shape[0], mid_count, lanes)
    apply_rows(s3, s2, u[2], starts, lanes, stride)


def hop_matrix(size, terms):
    row = lax.broadcasted_iota(jnp.int32, (size, size), 0)
    col = lax.broadcasted_iota(jnp.int32, (size, size), 1)
    gap = row ^ col
    total = jnp.zeros((size, size), f32)
    for lower, upper, weight in terms:
        differ = (lax.shift_right_logical(row, lower) & 1) != (
            lax.shift_right_logical(row, upper) & 1
        )
        total = total + jnp.where(differ & (gap == (1 << lower | 1 << upper)), weight, 0.0)
    return total


def flip_matrix(size, bit, side, weight):
    row = lax.broadcasted_iota(jnp.int32, (size, size), 0)
    col = lax.broadcasted_iota(jnp.int32, (size, size), 1)
    active = ((lax.shift_right_logical(row, bit) & 1) != side) & ((row ^ col) == (1 << bit))
    return jnp.where(active, weight, 0.0)


def main_kernel(
    n, mid_count, ranks, coef, mask, s3, s2, s1, s0, ut, u,
    adj, grads,
    xb, s4, yb, zb, rungs, chain, l4, l3, back, l2,
    part_a, part_b, got_a, got_b, sum_a, sum_b, full_a, full_b,
    sem_a, sem_x, sem_b, sem_r,
):
    me = lax.axis_index(AXIS)
    top_local, _, lanes = s3.shape
    top, low, _ = xb.shape
    rows = top * low
    low_bits = low.bit_length() - 1
    top_bits = top.bit_length() - 1
    lane_bits = lanes.bit_length() - 1
    flat = lambda ref: ref.reshape(rows, lanes)
    mid_flat = top_local * mid_count

    def each_peer(body):
        def step(d, carry):
            body(lax.rem(me + d, n))
            return carry
        lax.fori_loop(1, n, step, 0)

    barrier = pltpu.get_barrier_semaphore()
    each_peer(lambda peer: pl.semaphore_signal(barrier, inc=1, device_id={AXIS: peer}))
    pl.semaphore_wait(barrier, n - 1)

    def remote(src, dst, send, recv, peer):
        return pltpu.make_async_remote_copy(
            src_ref=src, dst_ref=dst, send_sem=send, recv_sem=recv, device_id={AXIS: peer}
        )

    def settle(ref, send, recv):
        whole = remote(ref, ref, send, recv, lax.rem(me + 1, n))
        whole.wait_recv()
        whole.wait_send()

    mine_rows = pl.ds(pl.multiple_of(me * top_local, top_local), top_local)
    mine_mid = pl.ds(pl.multiple_of(me * low, low), low)

    each_peer(
        lambda peer: remote(
            s3.at[:, pl.ds(pl.multiple_of(peer * low, low), low), :],
            xb.at[mine_rows], sem_a.at[0], sem_a.at[1], peer,
        ).start()
    )
    xb[mine_rows] = s3[:, mine_mid, :]

    weights = [coef[h] * mask[h].astype(f32) for h in range(coef.shape[0])]
    first_top = lane_bits + YQ
    first_rung = first_top + top_bits - 1
    lane_hops = split(hop_matrix(lanes, [(h, h + 1, weights[h]) for h in range(lane_bits - 1)]))
    top_hops = split(
        hop_matrix(top, [(k, k + 1, weights[first_top + k]) for k in range(top_bits - 1)])
    )
    flips = [
        [split(flip_matrix(top, k, side, weights[first_rung + k])) for side in range(2)]
        for k in range(low_bits)
    ]

    settle(xb.at[pl.ds(0, (n - 1) * top_local)], sem_a.at[0], sem_a.at[1])

    xf, s4f, l4f, l3f = flat(xb), s4, l4, flat(l3)
    near = [a * lanes for a in range(rows // lanes)]
    planes = list(range(low))
    apply_rows(s4f, xf, u[3], near, lanes, 1)
    u4 = split(u[4])
    inner = yb.shape[1:]
    for c in planes:
        yb[c] = dot3(u4, s4f[pl.ds(c, top, stride=low), :]).reshape(inner)

    copies = []
    own_bits = [lax.rem(me // (2**k), 2) for k in range(ranks)]

    def half(ref, k, side):
        where = (slice(None),) * (ranks - k) + (side,)
        return ref.at[where]

    def partner(k):
        return me + (1 - 2 * own_bits[k]) * 2**k

    for k in range(ranks - 1, -1, -1):
        copies.append(
            remote(half(yb, k, 1 - own_bits[k]), rungs.at[k], sem_x.at[0, k], sem_x.at[1, k],
                   partner(k))
        )
    half_low = low // 2
    copies.append(
        remote(
            yb.at[pl.ds((1 - own_bits[0]) * half_low, half_low)], chain,
            sem_x.at[0, ranks], sem_x.at[1, ranks], partner(0),
        )
    )
    for copy in copies:
        copy.start()

    lane = lax.broadcasted_iota(jnp.int32, (top, lanes), 1)
    lane_top = lax.shift_right_logical(lane, lane_bits - 1) & 1
    values = lambda c: yb[c].reshape(top, lanes)
    for c in planes:
        own = split(values(c))
        total = dot3(own, lane_hops) + dot3(top_hops, own)
        for k in range(low_bits):
            total = total + dot3(flips[k][c >> k & 1], values(c ^ 1 << k))
        for k in range(low_bits - 1):
            if (c >> k & 1) != (c >> (k + 1) & 1):
                total = total + weights[lane_bits + k] * values(c ^ 3 << k)
        rolled = pltpu.roll(values(c ^ 1), lanes // 2, 1)
        total = total + jnp.where(lane_top != (c & 1), weights[lane_bits - 1] * rolled, 0.0)
        zb[c] = total.reshape(inner)

    for copy in copies:
        copy.wait()
    for k in range(ranks):
        place = half(zb, k, 1 - own_bits[k])
        place[...] = place[...] + weights[first_rung + low_bits + k] * rungs[k]
    seat = pl.ds((1 - own_bits[0]) * half_low, half_low)
    zb[seat] = zb[seat] + weights[lane_bits + low_bits - 1] * chain[...]

    ut4 = split(ut[4])
    gram = None
    for c in planes:
        lam = split(zb[c].reshape(top, lanes))
        part = dot3(lam, s4f[pl.ds(c, top, stride=low), :], NT)
        gram = part if gram is None else gram + part
        l4f[pl.ds(c, top, stride=low), :] = dot3(ut4, lam)
    part_a[pl.ds(lanes, lanes), :] = gram
    apply_rows(l3f, l4f, ut[3], near, lanes, 1)

    each_peer(
        lambda peer: remote(
            l3.at[pl.ds(pl.multiple_of(peer * top_local, top_local), top_local)],
            back.at[:, mine_mid, :], sem_b.at[0], sem_b.at[1], peer,
        ).start()
    )
    back[:, mine_mid, :] = l3[mine_rows]
    part_a[pl.ds(0, lanes), :] = gram_rows(l4f, xf, near, lanes, 1)

    def scatter(part, got, chunk, number):
        each_peer(
            lambda peer: remote(
                part.at[pl.ds(pl.multiple_of(peer * chunk, 8), chunk)], got.at[me],
                sem_r.at[0, number], sem_r.at[1, number], peer,
            ).start()
        )
        got[me] = part[pl.ds(pl.multiple_of(me * chunk, 8), chunk), :]

    factor = 2.0 / (top * mid_count)

    def combine(part, got, mine, full, chunk, number):
        settle(got.at[pl.ds(0, n - 1)], sem_r.at[0, number], sem_r.at[1, number])
        mine[...] = factor * jnp.sum(got[...], axis=0)
        spot = pl.ds(pl.multiple_of(me * chunk, 8), chunk)
        each_peer(
            lambda peer: remote(
                mine, full.at[spot], sem_r.at[0, number + 1], sem_r.at[1, number + 1], peer
            ).start()
        )
        full[spot, :] = mine[...]

    def finish(full, chunk, number):
        settle(full.at[pl.ds(0, (n - 1) * chunk)], sem_r.at[0, number + 1], sem_r.at[1, number + 1])

    chunk_a = sum_a.shape[0]
    chunk_b = sum_b.shape[0]
    if n * chunk_a > 2 * lanes:
        part_a[pl.ds(2 * lanes, n * chunk_a - 2 * lanes), :] = jnp.zeros(
            (n * chunk_a - 2 * lanes, lanes), f32
        )
    if n * chunk_b > 3 * lanes:
        part_b[pl.ds(3 * lanes, n * chunk_b - 3 * lanes), :] = jnp.zeros(
            (n * chunk_b - 3 * lanes, lanes), f32
        )
    scatter(part_a, got_a, chunk_a, 0)

    low_part = pl.ds(0, (n - 1) * low)
    settle(back.at[:, low_part, :], sem_b.at[0], sem_b.at[1])
    backf = back.reshape(mid_flat, lanes)
    starts, stride = mid_starts(mid_flat, mid_count, lanes)
    part_b[pl.ds(2 * lanes, lanes), :] = gram_rows(backf, s2, starts, lanes, stride)
    apply_rows(l2, backf, ut[2], starts, lanes, stride)
    combine(part_a, got_a, sum_a, full_a, chunk_a, 0)
    wide = split(quads(l2))
    part_b[pl.ds(lanes, lanes), :] = gram_quads(wide, split(quads(s1)))
    apply_quads(l2, wide, u[1])
    part_b[pl.ds(0, lanes), :] = gram_lanes(l2, s0)
    scatter(part_b, got_b, chunk_b, 2)
    apply_lanes(adj, l2, u[0])
    combine(part_b, got_b, sum_b, full_b, chunk_b, 2)
    finish(full_a, chunk_a, 0)
    grads[pl.ds(3 * lanes, 2 * lanes), :] = full_a[pl.ds(0, 2 * lanes), :]
    finish(full_b, chunk_b, 2)
    grads[pl.ds(0, 3 * lanes), :] = full_b[pl.ds(0, 3 * lanes), :]


def on_device(initial_state, gate_angles, gate_pairs, hop_coef, hop_mask):
    top_local, mid_count, lanes = initial_state.shape
    blocks = gate_angles.shape[0]
    n = lax.axis_size(AXIS)
    top = top_local * n
    low = mid_count // n
    rows = top_local * mid_count
    ranks = (top // low).bit_length() - 1
    vmem = pl.BlockSpec(memory_space=pltpu.VMEM)
    smem = pl.BlockSpec(memory_space=pltpu.SMEM)
    flat = jax.ShapeDtypeStruct((rows, lanes), f32)
    gates = jax.ShapeDtypeStruct((blocks, lanes, lanes), f32)
    s0 = initial_state.reshape(rows, lanes)
    ut, u, s1, s2, s3 = pl.pallas_call(
        functools.partial(front_kernel, mid_count),
        out_shape=[gates, gates, flat, flat, flat],
        in_specs=[smem, vmem, vmem],
        out_specs=[vmem] * 5,
        name="front",
    )(gate_pairs, s0, gate_angles)
    s3 = s3.reshape(initial_state.shape)
    chunk_a = 8 * -(-2 * lanes // (8 * n))
    chunk_b = 8 * -(-3 * lanes // (8 * n))
    bits = (low,) + (2,) * ranks + (top >> ranks, lanes)
    half = (ranks, low) + (2,) * (ranks - 1) + (top >> ranks, lanes)
    full = (rows, lanes)
    tall = (top, low, lanes)
    adjoint, grads = pl.pallas_call(
        functools.partial(main_kernel, n, mid_count, ranks),
        out_shape=[flat, jax.ShapeDtypeStruct((blocks * lanes, lanes), f32)],
        in_specs=[smem, smem] + [vmem] * 6,
        out_specs=[vmem] * 2,
        scratch_shapes=[
            pltpu.VMEM(tall, f32),
            pltpu.VMEM(full, f32),
            pltpu.VMEM(bits, f32),
            pltpu.VMEM(bits, f32),
            pltpu.VMEM(half, f32),
            pltpu.VMEM((low // 2,) + bits[1:], f32),
            pltpu.VMEM(full, f32),
            pltpu.VMEM(tall, f32),
            pltpu.VMEM(initial_state.shape, f32),
            pltpu.VMEM(full, f32),
            pltpu.VMEM((n * chunk_a, lanes), f32),
            pltpu.VMEM((n * chunk_b, lanes), f32),
            pltpu.VMEM((n, chunk_a, lanes), f32),
            pltpu.VMEM((n, chunk_b, lanes), f32),
            pltpu.VMEM((chunk_a, lanes), f32),
            pltpu.VMEM((chunk_b, lanes), f32),
            pltpu.VMEM((n * chunk_a, lanes), f32),
            pltpu.VMEM((n * chunk_b, lanes), f32),
            pltpu.SemaphoreType.DMA((2,)),
            pltpu.SemaphoreType.DMA((2, ranks + 1)),
            pltpu.SemaphoreType.DMA((2,)),
            pltpu.SemaphoreType.DMA((2, 4)),
        ],
        compiler_params=pltpu.CompilerParams(collective_id=0, has_side_effects=True),
        name="main",
    )(hop_coef, hop_mask, s3, s2, s1, s0, ut, u)
    return adjoint.reshape(initial_state.shape), grads.reshape(blocks, lanes, lanes)


def solution(mesh):
    in_specs = (P(("runs", AXIS), None, None), P("runs", None), P(), P(), P())
    out_specs = (P(("runs", AXIS), None, None), P("runs", None, None))
    return jax.shard_map(
        on_device, mesh=mesh, in_specs=in_specs, out_specs=out_specs, check_vma=False
    )
```

```python
import functools
import jax
import jax.numpy as jnp
from jax import lax
from jax.experimental import pallas as pl
from jax.experimental.pallas import tpu as pltpu
from jax.sharding import PartitionSpec as P

YQ = 3
AXIS = "amp"
f32 = jnp.float32
bf16 = jnp.bfloat16
NN = ((1,), (0,))
NT = ((1,), (1,))
TN = ((0,), (0,))


def split(x):
    high = x.astype(bf16)
    return high, (x - high.astype(f32)).astype(bf16)


def dot_of(a, b, dims):
    return lax.dot_general(a, b, (dims, ((), ())), preferred_element_type=f32)


def dot3(a, b, dims=NN):
    ah, al = a if isinstance(a, tuple) else split(a)
    bh, bl = b if isinstance(b, tuple) else split(b)
    return dot_of(ah, bh, dims) + (dot_of(ah, bl, dims) + dot_of(al, bh, dims))


def rows_of(ref, start, size, stride):
    if stride == 1:
        return ref[pl.ds(start, size), :]
    return ref[pl.ds(start, size, stride=stride), :]


def put_rows(ref, start, size, stride, value):
    if stride == 1:
        ref[pl.ds(start, size), :] = value
    else:
        ref[pl.ds(start, size, stride=stride), :] = value


def apply_rows(dst, src, matrix, starts, size, stride):
    halves = split(matrix)
    for start in starts:
        put_rows(dst, start, size, stride, dot3(halves, rows_of(src, start, size, stride)))


def gram_rows(left, right, starts, size, stride, right_stride=None, right_starts=None):
    right_starts = starts if right_starts is None else right_starts
    right_stride = stride if right_stride is None else right_stride
    total = None
    for number in range(0, len(starts), 2):
        pick = range(number, min(number + 2, len(starts)))
        a = jnp.concatenate([rows_of(left, starts[i], size, stride) for i in pick], axis=1)
        b = jnp.concatenate(
            [rows_of(right, right_starts[i], size, right_stride) for i in pick], axis=1
        )
        part = dot3(a, b, NT)
        total = part if total is None else total + part
    return total


def apply_lanes(dst, src, matrix):
    rows = src.shape[0]
    halves = split(matrix)
    step = min(256, rows)
    for start in range(0, rows, step):
        dst[pl.ds(start, step), :] = dot3(src[pl.ds(start, step), :], halves)


def gram_lanes(left, right):
    rows = left.shape[0]
    total = None
    step = min(256, rows)
    for start in range(0, rows, step):
        part = dot3(left[pl.ds(start, step), :], right[pl.ds(start, step), :], TN)
        total = part if total is None else total + part
    return total


def spread_matrix(lanes):
    row = lax.broadcasted_iota(jnp.int32, (4 * lanes, lanes), 0)
    col = lax.broadcasted_iota(jnp.int32, (4 * lanes, lanes), 1)
    return jnp.where(lax.shift_right_logical(row, 2) == col, 1.0, 0.0).astype(bf16)


def same_low(lanes):
    row = lax.broadcasted_iota(jnp.int32, (4 * lanes, 4 * lanes), 0)
    col = lax.broadcasted_iota(jnp.int32, (4 * lanes, 4 * lanes), 1)
    return (row & 3) == (col & 3)


def widen(matrix):
    lanes = matrix.shape[0]
    spread = spread_matrix(lanes)
    keep = same_low(lanes)
    made = []
    for part in split(matrix):
        left = dot_of(spread, part, NN).astype(bf16)
        full = dot_of(left, spread, NT)
        made.append(jnp.where(keep, full, 0.0).astype(bf16))
    return tuple(made)


def quads(ref):
    count = ref.shape[0] // 4
    return jnp.concatenate([ref[pl.ds(q, count, stride=4), :] for q in range(4)], axis=1)


def apply_quads(dst, values, matrix):
    lanes = matrix.shape[0]
    result = dot3(values, widen(matrix))
    count = result.shape[0]
    for q in range(4):
        dst[pl.ds(q, count, stride=4), :] = result[:, q * lanes : (q + 1) * lanes]


def gram_quads(left, right):
    lanes = left[0].shape[1] // 4
    full = jnp.where(same_low(lanes), dot3(left, right, TN), 0.0)
    spread = spread_matrix(lanes)
    fh, fl = split(full)
    half = dot_of(fh, spread, NN) + dot_of(fl, spread, NN)
    hh, hl = split(half)
    return dot_of(spread, hh, TN) + dot_of(spread, hl, TN)


def mid_starts(rows, mid_count, lanes):
    stride = min(2 ** (YQ - 1), mid_count // lanes)
    groups = rows // (stride * lanes)
    return [g * stride * lanes + s for g in range(groups) for s in range(stride)], stride


def build_gates(pairs, cosines, sines, ut, u, which):
    lanes = ut.shape[1]
    givens = cosines.shape[1]
    lane = lax.broadcasted_iota(jnp.int32, (8, lanes), 1)
    row = lax.broadcasted_iota(jnp.int32, (lanes, lanes), 0)
    col = lax.broadcasted_iota(jnp.int32, (lanes, lanes), 1)
    for b in which:
        ut[b] = jnp.where(row == col, 1.0, 0.0)
    for g in range(givens):
        for b in which:
            p = pairs[b, 0, g]
            s = pairs[b, 1, g]
            low = lax.shift_right_logical(lane, p) & 1
            high = lax.shift_right_logical(lane, s) & 1
            cosine = jnp.broadcast_to(cosines[b : b + 1, g : g + 1], (8, lanes))
            sine = jnp.broadcast_to(sines[b : b + 1, g : g + 1], (8, lanes))
            keep = jnp.where(low != high, cosine, 1.0)[:1]
            up = jnp.where(low < high, -sine, 0.0)[:1]
            down = jnp.where(low > high, sine, 0.0)[:1]
            gap = lax.shift_left(jnp.int32(1), p) - lax.shift_left(jnp.int32(1), s)
            now = ut[b]
            ut[b] = (
                now * keep
                + pltpu.roll(now, (lanes - gap) & (lanes - 1), 1) * up
                + pltpu.roll(now, (lanes + gap) & (lanes - 1), 1) * down
            )
    for b in which:
        u[b] = jnp.transpose(ut[b])


def hop_matrix(size, terms):
    row = lax.broadcasted_iota(jnp.int32, (size, size), 0)
    col = lax.broadcasted_iota(jnp.int32, (size, size), 1)
    gap = row ^ col
    total = jnp.zeros((size, size), f32)
    for lower, upper, weight in terms:
        differ = (lax.shift_right_logical(row, lower) & 1) != (
            lax.shift_right_logical(row, upper) & 1
        )
        total = total + jnp.where(differ & (gap == (1 << lower | 1 << upper)), weight, 0.0)
    return total


def flip_matrix(size, bit, side, weight):
    row = lax.broadcasted_iota(jnp.int32, (size, size), 0)
    col = lax.broadcasted_iota(jnp.int32, (size, size), 1)
    active = ((lax.shift_right_logical(row, bit) & 1) != side) & ((row ^ col) == (1 << bit))
    return jnp.where(active, weight, 0.0)


def main_kernel(
    n, mid_count, ranks, pairs, coef, mask, angles, s0,
    adj, grads,
    ut, u, s1, s2, s3,
    xb, s4, yb, zb, rungs, chain, l4, l3, back, l2,
    part_a, part_b, got_a, got_b, sum_a, sum_b, full_a, full_b,
    sem_a, sem_x, sem_b, sem_r,
):
    me = lax.axis_index(AXIS)
    top_local, _, lanes = s3.shape
    top, low, _ = xb.shape
    rows = top * low
    low_bits = low.bit_length() - 1
    top_bits = top.bit_length() - 1
    lane_bits = lanes.bit_length() - 1
    flat = lambda ref: ref.reshape(rows, lanes)
    mid_flat = top_local * mid_count

    def each_peer(body):
        def step(d, carry):
            body(lax.rem(me + d, n))
            return carry
        lax.fori_loop(1, n, step, 0)

    barrier = pltpu.get_barrier_semaphore()
    each_peer(lambda peer: pl.semaphore_signal(barrier, inc=1, device_id={AXIS: peer}))

    cosines = jnp.cos(angles[...])
    sines = jnp.sin(angles[...])
    build_gates(pairs, cosines, sines, ut, u, (0, 1, 2))
    starts, stride = mid_starts(mid_flat, mid_count, lanes)
    apply_lanes(s1, s0, ut[0])
    apply_quads(s2, quads(s1), ut[1])
    apply_rows(s3.reshape(mid_flat, lanes), s2, u[2], starts, lanes, stride)
    pl.semaphore_wait(barrier, n - 1)

    def remote(src, dst, send, recv, peer):
        return pltpu.make_async_remote_copy(
            src_ref=src, dst_ref=dst, send_sem=send, recv_sem=recv, device_id={AXIS: peer}
        )

    def settle(ref, send, recv):
        whole = remote(ref, ref, send, recv, lax.rem(me + 1, n))
        whole.wait_recv()
        whole.wait_send()

    mine_rows = pl.ds(pl.multiple_of(me * top_local, top_local), top_local)
    mine_mid = pl.ds(pl.multiple_of(me * low, low), low)

    each_peer(
        lambda peer: remote(
            s3.at[:, pl.ds(pl.multiple_of(peer * low, low), low), :],
            xb.at[mine_rows], sem_a.at[0], sem_a.at[1], peer,
        ).start()
    )
    xb[mine_rows] = s3[:, mine_mid, :]

    build_gates(pairs, cosines, sines, ut, u, (3, 4))
    weights = [coef[h] * mask[h].astype(f32) for h in range(coef.shape[0])]
    first_top = lane_bits + YQ
    first_rung = first_top + top_bits - 1
    lane_hops = split(hop_matrix(lanes, [(h, h + 1, weights[h]) for h in range(lane_bits - 1)]))
    top_hops = split(
        hop_matrix(top, [(k, k + 1, weights[first_top + k]) for k in range(top_bits - 1)])
    )
    flips = [
        [split(flip_matrix(top, k, side, weights[first_rung + k])) for side in range(2)]
        for k in range(low_bits)
    ]

    settle(xb.at[pl.ds(0, (n - 1) * top_local)], sem_a.at[0], sem_a.at[1])

    xf, s4f, l4f, l3f = flat(xb), s4, l4, flat(l3)
    near = [a * lanes for a in range(rows // lanes)]
    planes = list(range(low))
    apply_rows(s4f, xf, u[3], near, lanes, 1)
    u4 = split(u[4])
    inner = yb.shape[1:]
    own_bits = [lax.rem(me // (2**k), 2) for k in range(ranks)]
    half_low = low // 2

    def half(ref, k, side):
        where = (slice(None),) * (ranks - 1 - k) + (side,)
        return ref.at[where]

    def partner(k):
        return me + (1 - 2 * own_bits[k]) * 2**k

    for c in planes:
        yb[c] = dot3(u4, s4f[pl.ds(c, top, stride=low), :]).reshape(inner)
        for k in range(ranks - 1, -1, -1):
            remote(
                half(yb.at[c], k, 1 - own_bits[k]), rungs.at[k, c],
                sem_x.at[0, k], sem_x.at[1, k], partner(k),
            ).start()
    remote(
        yb.at[pl.ds((1 - own_bits[0]) * half_low, half_low)], chain,
        sem_x.at[0, ranks], sem_x.at[1, ranks], partner(0),
    ).start()

    lane = lax.broadcasted_iota(jnp.int32, (top, lanes), 1)
    lane_top = lax.shift_right_logical(lane, lane_bits - 1) & 1
    values = lambda c: yb[c].reshape(top, lanes)
    for c in planes:
        own = split(values(c))
        total = dot3(own, lane_hops) + dot3(top_hops, own)
        for k in range(low_bits):
            total = total + dot3(flips[k][c >> k & 1], values(c ^ 1 << k))
        for k in range(low_bits - 1):
            if (c >> k & 1) != (c >> (k + 1) & 1):
                total = total + weights[lane_bits + k] * values(c ^ 3 << k)
        rolled = pltpu.roll(values(c ^ 1), lanes // 2, 1)
        total = total + jnp.where(lane_top != (c & 1), weights[lane_bits - 1] * rolled, 0.0)
        zb[c] = total.reshape(inner)

    seat = pl.ds((1 - own_bits[0]) * half_low, half_low)
    settle(chain, sem_x.at[0, ranks], sem_x.at[1, ranks])
    zb[seat] = zb[seat] + weights[lane_bits + low_bits - 1] * chain[...]
    for k in range(ranks):
        settle(rungs.at[k], sem_x.at[0, k], sem_x.at[1, k])
        for c in planes:
            place = half(zb.at[c], k, 1 - own_bits[k])
            place[...] = place[...] + weights[first_rung + low_bits + k] * rungs[k, c]

    ut4 = split(ut[4])
    for c in planes:
        l4f[pl.ds(c, top, stride=low), :] = dot3(ut4, zb[c].reshape(top, lanes))
    apply_rows(l3f, l4f, ut[3], near, lanes, 1)

    each_peer(
        lambda peer: remote(
            l3.at[pl.ds(pl.multiple_of(peer * top_local, top_local), top_local)],
            back.at[:, mine_mid, :], sem_b.at[0], sem_b.at[1], peer,
        ).start()
    )
    back[:, mine_mid, :] = l3[mine_rows]
    gram = None
    for c in range(0, low, 2):
        lam = jnp.concatenate([zb[c + i].reshape(top, lanes) for i in range(2)], axis=1)
        old = jnp.concatenate(
            [s4f[pl.ds(c + i, top, stride=low), :] for i in range(2)], axis=1
        )
        part = dot3(lam, old, NT)
        gram = part if gram is None else gram + part
    part_a[pl.ds(lanes, lanes), :] = gram
    part_a[pl.ds(0, lanes), :] = gram_rows(l4f, xf, near, lanes, 1)

    def scatter(part, got, chunk, number):
        each_peer(
            lambda peer: remote(
                part.at[pl.ds(pl.multiple_of(peer * chunk, 8), chunk)], got.at[me],
                sem_r.at[0, number], sem_r.at[1, number], peer,
            ).start()
        )
        got[me] = part[pl.ds(pl.multiple_of(me * chunk, 8), chunk), :]

    factor = 2.0 / (top * mid_count)

    def combine(part, got, mine, full, chunk, number):
        settle(got.at[pl.ds(0, n - 1)], sem_r.at[0, number], sem_r.at[1, number])
        mine[...] = factor * jnp.sum(got[...], axis=0)
        spot = pl.ds(pl.multiple_of(me * chunk, 8), chunk)
        each_peer(
            lambda peer: remote(
                mine, full.at[spot], sem_r.at[0, number + 1], sem_r.at[1, number + 1], peer
            ).start()
        )
        full[spot, :] = mine[...]

    def finish(full, chunk, number):
        settle(full.at[pl.ds(0, (n - 1) * chunk)], sem_r.at[0, number + 1], sem_r.at[1, number + 1])

    chunk_a = sum_a.shape[0]
    chunk_b = sum_b.shape[0]
    if n * chunk_a > 2 * lanes:
        part_a[pl.ds(2 * lanes, n * chunk_a - 2 * lanes), :] = jnp.zeros(
            (n * chunk_a - 2 * lanes, lanes), f32
        )
    if n * chunk_b > 3 * lanes:
        part_b[pl.ds(3 * lanes, n * chunk_b - 3 * lanes), :] = jnp.zeros(
            (n * chunk_b - 3 * lanes, lanes), f32
        )
    scatter(part_a, got_a, chunk_a, 0)

    low_part = pl.ds(0, (n - 1) * low)
    settle(back.at[:, low_part, :], sem_b.at[0], sem_b.at[1])
    backf = back.reshape(mid_flat, lanes)
    part_b[pl.ds(2 * lanes, lanes), :] = gram_rows(backf, s2, starts, lanes, stride)
    apply_rows(l2, backf, ut[2], starts, lanes, stride)
    combine(part_a, got_a, sum_a, full_a, chunk_a, 0)
    wide = split(quads(l2))
    part_b[pl.ds(lanes, lanes), :] = gram_quads(wide, split(quads(s1)))
    apply_quads(l2, wide, u[1])
    part_b[pl.ds(0, lanes), :] = gram_lanes(l2, s0)
    scatter(part_b, got_b, chunk_b, 2)
    apply_lanes(adj, l2, u[0])
    combine(part_b, got_b, sum_b, full_b, chunk_b, 2)
    finish(full_a, chunk_a, 0)
    grads[pl.ds(3 * lanes, 2 * lanes), :] = full_a[pl.ds(0, 2 * lanes), :]
    finish(full_b, chunk_b, 2)
    grads[pl.ds(0, 3 * lanes), :] = full_b[pl.ds(0, 3 * lanes), :]


def on_device(initial_state, gate_angles, gate_pairs, hop_coef, hop_mask):
    top_local, mid_count, lanes = initial_state.shape
    blocks = gate_angles.shape[0]
    n = lax.axis_size(AXIS)
    top = top_local * n
    low = mid_count // n
    rows = top_local * mid_count
    ranks = (top // low).bit_length() - 1
    vmem = pl.BlockSpec(memory_space=pltpu.VMEM)
    smem = pl.BlockSpec(memory_space=pltpu.SMEM)
    flat = jax.ShapeDtypeStruct((rows, lanes), f32)
    gates = (blocks, lanes, lanes)
    s0 = initial_state.reshape(rows, lanes)
    chunk_a = 8 * -(-2 * lanes // (8 * n))
    chunk_b = 8 * -(-3 * lanes // (8 * n))
    bits = (low,) + (2,) * ranks + (top >> ranks, lanes)
    half = (ranks, low) + (2,) * (ranks - 1) + (top >> ranks, lanes)
    full = (rows, lanes)
    tall = (top, low, lanes)
    adjoint, grads = pl.pallas_call(
        functools.partial(main_kernel, n, mid_count, ranks),
        out_shape=[flat, jax.ShapeDtypeStruct((blocks * lanes, lanes), f32)],
        in_specs=[smem] * 3 + [vmem] * 2,
        out_specs=[vmem] * 2,
        scratch_shapes=[
            pltpu.VMEM(gates, f32),
            pltpu.VMEM(gates, f32),
            pltpu.VMEM(full, f32),
            pltpu.VMEM(full, f32),
            pltpu.VMEM(initial_state.shape, f32),
            pltpu.VMEM(tall, f32),
            pltpu.VMEM(full, f32),
            pltpu.VMEM(bits, f32),
            pltpu.VMEM(bits, f32),
            pltpu.VMEM(half, f32),
            pltpu.VMEM((low // 2,) + bits[1:], f32),
            pltpu.VMEM(full, f32),
            pltpu.VMEM(tall, f32),
            pltpu.VMEM(initial_state.shape, f32),
            pltpu.VMEM(full, f32),
            pltpu.VMEM((n * chunk_a, lanes), f32),
            pltpu.VMEM((n * chunk_b, lanes), f32),
            pltpu.VMEM((n, chunk_a, lanes), f32),
            pltpu.VMEM((n, chunk_b, lanes), f32),
            pltpu.VMEM((chunk_a, lanes), f32),
            pltpu.VMEM((chunk_b, lanes), f32),
            pltpu.VMEM((n * chunk_a, lanes), f32),
            pltpu.VMEM((n * chunk_b, lanes), f32),
            pltpu.SemaphoreType.DMA((2,)),
            pltpu.SemaphoreType.DMA((2, ranks + 1)),
            pltpu.SemaphoreType.DMA((2,)),
            pltpu.SemaphoreType.DMA((2, 4)),
        ],
        compiler_params=pltpu.CompilerParams(collective_id=0, has_side_effects=True),
        name="main",
    )(jnp.transpose(gate_pairs, (0, 2, 1)), hop_coef, hop_mask, gate_angles, s0)
    return adjoint.reshape(initial_state.shape), grads.reshape(blocks, lanes, lanes)


def solution(mesh):
    in_specs = (P(("runs", AXIS), None, None), P("runs", None), P(), P(), P())
    out_specs = (P(("runs", AXIS), None, None), P("runs", None, None))
    return jax.shard_map(
        on_device, mesh=mesh, in_specs=in_specs, out_specs=out_specs, check_vma=False
    )
```

```python
import functools
import jax
import jax.numpy as jnp
from jax import lax
from jax.experimental import pallas as pl
from jax.experimental.pallas import tpu as pltpu
from jax.sharding import PartitionSpec as P

YQ = 3
AXIS = "amp"
f32 = jnp.float32
bf16 = jnp.bfloat16
NN = ((1,), (0,))
NT = ((1,), (1,))
TN = ((0,), (0,))


def split(x):
    high = x.astype(bf16)
    return high, (x - high.astype(f32)).astype(bf16)


def dot_of(a, b, dims):
    return lax.dot_general(a, b, (dims, ((), ())), preferred_element_type=f32)


def dot3(a, b, dims=NN):
    ah, al = a if isinstance(a, tuple) else split(a)
    bh, bl = b if isinstance(b, tuple) else split(b)
    return dot_of(ah, bh, dims) + (dot_of(ah, bl, dims) + dot_of(al, bh, dims))


def rows_of(ref, start, size, stride):
    if stride == 1:
        return ref[pl.ds(start, size), :]
    return ref[pl.ds(start, size, stride=stride), :]


def put_rows(ref, start, size, stride, value):
    if stride == 1:
        ref[pl.ds(start, size), :] = value
    else:
        ref[pl.ds(start, size, stride=stride), :] = value


def apply_rows(dst, src, matrix, starts, size, stride):
    halves = split(matrix)
    for start in starts:
        put_rows(dst, start, size, stride, dot3(halves, rows_of(src, start, size, stride)))


def gram_rows(left, right, starts, size, stride, right_stride=None, right_starts=None):
    right_starts = starts if right_starts is None else right_starts
    right_stride = stride if right_stride is None else right_stride
    total = None
    for number in range(0, len(starts), 2):
        pick = range(number, min(number + 2, len(starts)))
        a = jnp.concatenate([rows_of(left, starts[i], size, stride) for i in pick], axis=1)
        b = jnp.concatenate(
            [rows_of(right, right_starts[i], size, right_stride) for i in pick], axis=1
        )
        part = dot3(a, b, NT)
        total = part if total is None else total + part
    return total


def apply_lanes(dst, src, matrix):
    rows = src.shape[0]
    halves = split(matrix)
    step = min(256, rows)
    for start in range(0, rows, step):
        dst[pl.ds(start, step), :] = dot3(src[pl.ds(start, step), :], halves)


def gram_lanes(left, right):
    rows = left.shape[0]
    total = None
    step = min(256, rows)
    for start in range(0, rows, step):
        part = dot3(left[pl.ds(start, step), :], right[pl.ds(start, step), :], TN)
        total = part if total is None else total + part
    return total


def spread_matrix(lanes):
    row = lax.broadcasted_iota(jnp.int32, (4 * lanes, lanes), 0)
    col = lax.broadcasted_iota(jnp.int32, (4 * lanes, lanes), 1)
    return jnp.where(lax.shift_right_logical(row, 2) == col, 1.0, 0.0).astype(bf16)


def same_low(lanes):
    row = lax.broadcasted_iota(jnp.int32, (4 * lanes, 4 * lanes), 0)
    col = lax.broadcasted_iota(jnp.int32, (4 * lanes, 4 * lanes), 1)
    return (row & 3) == (col & 3)


def widen(matrix):
    lanes = matrix.shape[0]
    spread = spread_matrix(lanes)
    keep = same_low(lanes)
    made = []
    for part in split(matrix):
        left = dot_of(spread, part, NN).astype(bf16)
        full = dot_of(left, spread, NT)
        made.append(jnp.where(keep, full, 0.0).astype(bf16))
    return tuple(made)


def quads(ref):
    count = ref.shape[0] // 4
    return jnp.concatenate([ref[pl.ds(q, count, stride=4), :] for q in range(4)], axis=1)


def apply_quads(dst, values, matrix):
    lanes = matrix.shape[0]
    result = dot3(values, widen(matrix))
    count = result.shape[0]
    for q in range(4):
        dst[pl.ds(q, count, stride=4), :] = result[:, q * lanes : (q + 1) * lanes]


def gram_quads(left, right):
    lanes = left[0].shape[1] // 4
    full = jnp.where(same_low(lanes), dot3(left, right, TN), 0.0)
    spread = spread_matrix(lanes)
    fh, fl = split(full)
    half = dot_of(fh, spread, NN) + dot_of(fl, spread, NN)
    hh, hl = split(half)
    return dot_of(spread, hh, TN) + dot_of(spread, hl, TN)


def mid_starts(rows, mid_count, lanes):
    stride = min(2 ** (YQ - 1), mid_count // lanes)
    groups = rows // (stride * lanes)
    return [g * stride * lanes + s for g in range(groups) for s in range(stride)], stride


def build_gates(pairs, cosines, sines, ut, u, which):
    lanes = ut.shape[1]
    givens = cosines.shape[1]
    lane = lax.broadcasted_iota(jnp.int32, (8, lanes), 1)
    row = lax.broadcasted_iota(jnp.int32, (lanes, lanes), 0)
    col = lax.broadcasted_iota(jnp.int32, (lanes, lanes), 1)
    for b in which:
        ut[b] = jnp.where(row == col, 1.0, 0.0)
    for g in range(givens):
        for b in which:
            p = pairs[b, 0, g]
            s = pairs[b, 1, g]
            low = lax.shift_right_logical(lane, p) & 1
            high = lax.shift_right_logical(lane, s) & 1
            cosine = jnp.broadcast_to(cosines[b : b + 1, g : g + 1], (8, lanes))
            sine = jnp.broadcast_to(sines[b : b + 1, g : g + 1], (8, lanes))
            keep = jnp.where(low != high, cosine, 1.0)[:1]
            up = jnp.where(low < high, -sine, 0.0)[:1]
            down = jnp.where(low > high, sine, 0.0)[:1]
            gap = lax.shift_left(jnp.int32(1), p) - lax.shift_left(jnp.int32(1), s)
            now = ut[b]
            ut[b] = (
                now * keep
                + pltpu.roll(now, (lanes - gap) & (lanes - 1), 1) * up
                + pltpu.roll(now, (lanes + gap) & (lanes - 1), 1) * down
            )
    for b in which:
        u[b] = jnp.transpose(ut[b])


def hop_matrix(size, terms):
    row = lax.broadcasted_iota(jnp.int32, (size, size), 0)
    col = lax.broadcasted_iota(jnp.int32, (size, size), 1)
    gap = row ^ col
    total = jnp.zeros((size, size), f32)
    for lower, upper, weight in terms:
        differ = (lax.shift_right_logical(row, lower) & 1) != (
            lax.shift_right_logical(row, upper) & 1
        )
        total = total + jnp.where(differ & (gap == (1 << lower | 1 << upper)), weight, 0.0)
    return total


def flip_matrix(size, bit, side, weight):
    row = lax.broadcasted_iota(jnp.int32, (size, size), 0)
    col = lax.broadcasted_iota(jnp.int32, (size, size), 1)
    active = ((lax.shift_right_logical(row, bit) & 1) != side) & ((row ^ col) == (1 << bit))
    return jnp.where(active, weight, 0.0)


def main_kernel(
    n, mid_count, ranks, pairs, coef, mask, angles, s0,
    adj, grads,
    ut, u, s1, s2, s3,
    xb, s4, yb, zb, rungs, chain, l4, l3, back, l2,
    part_a, part_b, lent_a, lent_b, got_a, got_b, sum_a, sum_b, full_a, full_b,
    sem_a, sem_x, sem_b, sem_r,
):
    me = lax.axis_index(AXIS)
    top_local, _, lanes = s3.shape
    top, low, _ = xb.shape
    rows = top * low
    low_bits = low.bit_length() - 1
    top_bits = top.bit_length() - 1
    lane_bits = lanes.bit_length() - 1
    flat = lambda ref: ref.reshape(rows, lanes)
    mid_flat = top_local * mid_count

    def each_peer(body):
        def step(d, carry):
            body(lax.rem(me + d, n))
            return carry
        lax.fori_loop(1, n, step, 0)

    barrier = pltpu.get_barrier_semaphore()
    each_peer(lambda peer: pl.semaphore_signal(barrier, inc=1, device_id={AXIS: peer}))

    cosines = jnp.cos(angles[...])
    sines = jnp.sin(angles[...])
    build_gates(pairs, cosines, sines, ut, u, (0, 1, 2))
    starts, stride = mid_starts(mid_flat, mid_count, lanes)
    apply_lanes(s1, s0, ut[0])
    apply_quads(s2, quads(s1), ut[1])
    apply_rows(s3.reshape(mid_flat, lanes), s2, u[2], starts, lanes, stride)
    pl.semaphore_wait(barrier, n - 1)

    def remote(src, dst, send, recv, peer):
        return pltpu.make_async_remote_copy(
            src_ref=src, dst_ref=dst, send_sem=send, recv_sem=recv, device_id={AXIS: peer}
        )

    def settle(ref, send, recv):
        whole = remote(ref, ref, send, recv, lax.rem(me + 1, n))
        whole.wait_recv()
        whole.wait_send()

    mine_rows = pl.ds(pl.multiple_of(me * top_local, top_local), top_local)
    mine_mid = pl.ds(pl.multiple_of(me * low, low), low)

    each_peer(
        lambda peer: remote(
            s3.at[:, pl.ds(pl.multiple_of(peer * low, low), low), :],
            xb.at[mine_rows], sem_a.at[0], sem_a.at[1], peer,
        ).start()
    )
    xb[mine_rows] = s3[:, mine_mid, :]

    build_gates(pairs, cosines, sines, ut, u, (3, 4))
    weights = [coef[h] * mask[h].astype(f32) for h in range(coef.shape[0])]
    first_top = lane_bits + YQ
    first_rung = first_top + top_bits - 1
    lane_hops = split(hop_matrix(lanes, [(h, h + 1, weights[h]) for h in range(lane_bits - 1)]))
    top_hops = split(
        hop_matrix(top, [(k, k + 1, weights[first_top + k]) for k in range(top_bits - 1)])
    )
    flips = [
        [split(flip_matrix(top, k, side, weights[first_rung + k])) for side in range(2)]
        for k in range(low_bits)
    ]

    settle(xb.at[pl.ds(0, (n - 1) * top_local)], sem_a.at[0], sem_a.at[1])

    xf, s4f, l4f, l3f = flat(xb), s4, l4, flat(l3)
    near = [a * lanes for a in range(rows // lanes)]
    planes = list(range(low))
    apply_rows(s4f, xf, u[3], near, lanes, 1)
    u4 = split(u[4])
    inner = yb.shape[1:]
    own_bits = [lax.rem(me // (2**k), 2) for k in range(ranks)]
    half_low = low // 2

    def half(ref, k, side):
        where = (slice(None),) * (ranks - 1 - k) + (side,)
        return ref.at[where]

    def partner(k):
        return me + (1 - 2 * own_bits[k]) * 2**k

    for c in planes:
        yb[c] = dot3(u4, s4f[pl.ds(c, top, stride=low), :]).reshape(inner)
        for k in range(ranks - 1, -1, -1):
            remote(
                half(yb.at[c], k, 1 - own_bits[k]), rungs.at[k, c],
                sem_x.at[0, k], sem_x.at[1, k], partner(k),
            ).start()
    remote(
        yb.at[pl.ds((1 - own_bits[0]) * half_low, half_low)], chain,
        sem_x.at[0, ranks], sem_x.at[1, ranks], partner(0),
    ).start()

    lane = lax.broadcasted_iota(jnp.int32, (top, lanes), 1)
    lane_top = lax.shift_right_logical(lane, lane_bits - 1) & 1
    values = lambda c: yb[c].reshape(top, lanes)
    for c in planes:
        own = split(values(c))
        total = dot3(own, lane_hops) + dot3(top_hops, own)
        for k in range(low_bits):
            total = total + dot3(flips[k][c >> k & 1], values(c ^ 1 << k))
        for k in range(low_bits - 1):
            if (c >> k & 1) != (c >> (k + 1) & 1):
                total = total + weights[lane_bits + k] * values(c ^ 3 << k)
        rolled = pltpu.roll(values(c ^ 1), lanes // 2, 1)
        total = total + jnp.where(lane_top != (c & 1), weights[lane_bits - 1] * rolled, 0.0)
        zb[c] = total.reshape(inner)

    seat = pl.ds((1 - own_bits[0]) * half_low, half_low)
    settle(chain, sem_x.at[0, ranks], sem_x.at[1, ranks])
    zb[seat] = zb[seat] + weights[lane_bits + low_bits - 1] * chain[...]
    for k in range(ranks):
        settle(rungs.at[k], sem_x.at[0, k], sem_x.at[1, k])
        for c in planes:
            place = half(zb.at[c], k, 1 - own_bits[k])
            place[...] = place[...] + weights[first_rung + low_bits + k] * rungs[k, c]

    ut4 = split(ut[4])
    for c in planes:
        l4f[pl.ds(c, top, stride=low), :] = dot3(ut4, zb[c].reshape(top, lanes))
    apply_rows(l3f, l4f, ut[3], near, lanes, 1)

    each_peer(
        lambda peer: remote(
            l3.at[pl.ds(pl.multiple_of(peer * top_local, top_local), top_local)],
            back.at[:, mine_mid, :], sem_b.at[0], sem_b.at[1], peer,
        ).start()
    )
    back[:, mine_mid, :] = l3[mine_rows]
    gram = None
    for c in range(0, low, 2):
        lam = jnp.concatenate([zb[c + i].reshape(top, lanes) for i in range(2)], axis=1)
        old = jnp.concatenate(
            [s4f[pl.ds(c + i, top, stride=low), :] for i in range(2)], axis=1
        )
        part = dot3(lam, old, NT)
        gram = part if gram is None else gram + part
    part_a[pl.ds(lanes, lanes), :] = gram
    part_a[pl.ds(0, lanes), :] = gram_rows(l4f, xf, near, lanes, 1)

    factor = 2.0 / (top * mid_count)
    mate = partner(0)
    pairs_of = n // 2

    def each_twin(body):
        def step(d, carry):
            body(lax.rem(me + 2 * d, n))
            return carry
        lax.fori_loop(1, pairs_of, step, 0)

    def own_half(chunk, side):
        size = pairs_of * chunk
        return pl.ds(pl.multiple_of(side * size, 8), size)

    def lend(part, lent, chunk, number):
        remote(
            part.at[own_half(chunk, 1 - own_bits[0])], lent,
            sem_r.at[0, number], sem_r.at[1, number], mate,
        ).start()

    def scatter(part, lent, got, chunk, number):
        settle(lent, sem_r.at[0, number], sem_r.at[1, number])
        lent[...] = lent[...] + part[own_half(chunk, own_bits[0]), :]
        each_twin(
            lambda peer: remote(
                lent.at[pl.ds(pl.multiple_of(peer // 2 * chunk, 8), chunk)], got.at[me // 2],
                sem_r.at[0, number + 1], sem_r.at[1, number + 1], peer,
            ).start()
        )
        got[me // 2] = lent[pl.ds(pl.multiple_of(me // 2 * chunk, 8), chunk), :]

    def combine(got, mine, full, chunk, number):
        settle(got.at[pl.ds(0, pairs_of - 1)], sem_r.at[0, number + 1], sem_r.at[1, number + 1])
        mine[...] = factor * jnp.sum(got[...], axis=0)
        spot = pl.ds(
            pl.multiple_of(own_bits[0] * pairs_of * chunk + me // 2 * chunk, 8), chunk
        )
        each_twin(
            lambda peer: remote(
                mine, full.at[spot], sem_r.at[0, number + 2], sem_r.at[1, number + 2], peer
            ).start()
        )
        full[spot, :] = mine[...]

    def trade(full, chunk, number):
        settle(
            full.at[pl.ds(0, (pairs_of - 1) * chunk)],
            sem_r.at[0, number + 2], sem_r.at[1, number + 2],
        )
        whole = full.at[own_half(chunk, own_bits[0])]
        remote(whole, whole, sem_r.at[0, number + 3], sem_r.at[1, number + 3], mate).start()

    def finish(full, chunk, number):
        settle(
            full.at[pl.ds(0, pairs_of * chunk)],
            sem_r.at[0, number + 3], sem_r.at[1, number + 3],
        )

    chunk_a = sum_a.shape[0]
    chunk_b = sum_b.shape[0]
    if n * chunk_a > 2 * lanes:
        part_a[pl.ds(2 * lanes, n * chunk_a - 2 * lanes), :] = jnp.zeros(
            (n * chunk_a - 2 * lanes, lanes), f32
        )
    if n * chunk_b > 3 * lanes:
        part_b[pl.ds(3 * lanes, n * chunk_b - 3 * lanes), :] = jnp.zeros(
            (n * chunk_b - 3 * lanes, lanes), f32
        )
    lend(part_a, lent_a, chunk_a, 0)
    scatter(part_a, lent_a, got_a, chunk_a, 0)

    low_part = pl.ds(0, (n - 1) * low)
    settle(back.at[:, low_part, :], sem_b.at[0], sem_b.at[1])
    backf = back.reshape(mid_flat, lanes)
    apply_rows(l2, backf, ut[2], starts, lanes, stride)
    part_b[pl.ds(2 * lanes, lanes), :] = gram_rows(backf, s2, starts, lanes, stride)
    combine(got_a, sum_a, full_a, chunk_a, 0)
    wide = split(quads(l2))
    part_b[pl.ds(lanes, lanes), :] = gram_quads(wide, split(quads(s1)))
    apply_quads(l2, wide, u[1])
    part_b[pl.ds(0, lanes), :] = gram_lanes(l2, s0)
    lend(part_b, lent_b, chunk_b, 4)
    trade(full_a, chunk_a, 0)
    scatter(part_b, lent_b, got_b, chunk_b, 4)
    apply_lanes(adj, l2, u[0])
    finish(full_a, chunk_a, 0)
    grads[pl.ds(3 * lanes, 2 * lanes), :] = full_a[pl.ds(0, 2 * lanes), :]
    combine(got_b, sum_b, full_b, chunk_b, 4)
    trade(full_b, chunk_b, 4)
    finish(full_b, chunk_b, 4)
    grads[pl.ds(0, 3 * lanes), :] = full_b[pl.ds(0, 3 * lanes), :]


def on_device(initial_state, gate_angles, gate_pairs, hop_coef, hop_mask):
    top_local, mid_count, lanes = initial_state.shape
    blocks = gate_angles.shape[0]
    n = lax.axis_size(AXIS)
    top = top_local * n
    low = mid_count // n
    rows = top_local * mid_count
    ranks = (top // low).bit_length() - 1
    vmem = pl.BlockSpec(memory_space=pltpu.VMEM)
    smem = pl.BlockSpec(memory_space=pltpu.SMEM)
    flat = jax.ShapeDtypeStruct((rows, lanes), f32)
    gates = (blocks, lanes, lanes)
    s0 = initial_state.reshape(rows, lanes)
    chunk_a = 8 * -(-2 * lanes // (8 * n))
    chunk_b = 8 * -(-3 * lanes // (8 * n))
    bits = (low,) + (2,) * ranks + (top >> ranks, lanes)
    half = (ranks, low) + (2,) * (ranks - 1) + (top >> ranks, lanes)
    full = (rows, lanes)
    tall = (top, low, lanes)
    adjoint, grads = pl.pallas_call(
        functools.partial(main_kernel, n, mid_count, ranks),
        out_shape=[flat, jax.ShapeDtypeStruct((blocks * lanes, lanes), f32)],
        in_specs=[smem] * 3 + [vmem] * 2,
        out_specs=[vmem] * 2,
        scratch_shapes=[
            pltpu.VMEM(gates, f32),
            pltpu.VMEM(gates, f32),
            pltpu.VMEM(full, f32),
            pltpu.VMEM(full, f32),
            pltpu.VMEM(initial_state.shape, f32),
            pltpu.VMEM(tall, f32),
            pltpu.VMEM(full, f32),
            pltpu.VMEM(bits, f32),
            pltpu.VMEM(bits, f32),
            pltpu.VMEM(half, f32),
            pltpu.VMEM((low // 2,) + bits[1:], f32),
            pltpu.VMEM(full, f32),
            pltpu.VMEM(tall, f32),
            pltpu.VMEM(initial_state.shape, f32),
            pltpu.VMEM(full, f32),
            pltpu.VMEM((n * chunk_a, lanes), f32),
            pltpu.VMEM((n * chunk_b, lanes), f32),
            pltpu.VMEM((n // 2 * chunk_a, lanes), f32),
            pltpu.VMEM((n // 2 * chunk_b, lanes), f32),
            pltpu.VMEM((n // 2, chunk_a, lanes), f32),
            pltpu.VMEM((n // 2, chunk_b, lanes), f32),
            pltpu.VMEM((chunk_a, lanes), f32),
            pltpu.VMEM((chunk_b, lanes), f32),
            pltpu.VMEM((n * chunk_a, lanes), f32),
            pltpu.VMEM((n * chunk_b, lanes), f32),
            pltpu.SemaphoreType.DMA((2,)),
            pltpu.SemaphoreType.DMA((2, ranks + 1)),
            pltpu.SemaphoreType.DMA((2,)),
            pltpu.SemaphoreType.DMA((2, 8)),
        ],
        compiler_params=pltpu.CompilerParams(collective_id=0, has_side_effects=True),
        name="main",
    )(jnp.transpose(gate_pairs, (0, 2, 1)), hop_coef, hop_mask, gate_angles, s0)
    return adjoint.reshape(initial_state.shape), grads.reshape(blocks, lanes, lanes)


def solution(mesh):
    in_specs = (P(("runs", AXIS), None, None), P("runs", None), P(), P(), P())
    out_specs = (P(("runs", AXIS), None, None), P("runs", None, None))
    return jax.shard_map(
        on_device, mesh=mesh, in_specs=in_specs, out_specs=out_specs, check_vma=False
    )
```

```python
import functools
import jax
import jax.numpy as jnp
from jax import lax
from jax.experimental import pallas as pl
from jax.experimental.pallas import tpu as pltpu
from jax.sharding import PartitionSpec as P

YQ = 3
AXIS = "amp"
f32 = jnp.float32
bf16 = jnp.bfloat16
NN = ((1,), (0,))
NT = ((1,), (1,))
TN = ((0,), (0,))


def split(x):
    high = x.astype(bf16)
    return high, (x - high.astype(f32)).astype(bf16)


def dot_of(a, b, dims):
    return lax.dot_general(a, b, (dims, ((), ())), preferred_element_type=f32)


def dot3(a, b, dims=NN):
    ah, al = a if isinstance(a, tuple) else split(a)
    bh, bl = b if isinstance(b, tuple) else split(b)
    return dot_of(ah, bh, dims) + (dot_of(ah, bl, dims) + dot_of(al, bh, dims))


def rows_of(ref, start, size, stride):
    if stride == 1:
        return ref[pl.ds(start, size), :]
    return ref[pl.ds(start, size, stride=stride), :]


def put_rows(ref, start, size, stride, value):
    if stride == 1:
        ref[pl.ds(start, size), :] = value
    else:
        ref[pl.ds(start, size, stride=stride), :] = value


def apply_rows(dst, src, matrix, starts, size, stride):
    halves = split(matrix)
    for start in starts:
        put_rows(dst, start, size, stride, dot3(halves, rows_of(src, start, size, stride)))


def gram_rows(left, right, starts, size, stride, right_stride=None, right_starts=None):
    right_starts = starts if right_starts is None else right_starts
    right_stride = stride if right_stride is None else right_stride
    total = None
    for number in range(0, len(starts), 2):
        pick = range(number, min(number + 2, len(starts)))
        a = jnp.concatenate([rows_of(left, starts[i], size, stride) for i in pick], axis=1)
        b = jnp.concatenate(
            [rows_of(right, right_starts[i], size, right_stride) for i in pick], axis=1
        )
        part = dot3(a, b, NT)
        total = part if total is None else total + part
    return total


def apply_lanes(dst, src, matrix):
    rows = src.shape[0]
    halves = split(matrix)
    step = min(256, rows)
    for start in range(0, rows, step):
        dst[pl.ds(start, step), :] = dot3(src[pl.ds(start, step), :], halves)


def gram_lanes(left, right):
    rows = left.shape[0]
    total = None
    step = min(256, rows)
    for start in range(0, rows, step):
        part = dot3(left[pl.ds(start, step), :], right[pl.ds(start, step), :], TN)
        total = part if total is None else total + part
    return total


def spread_matrix(lanes):
    row = lax.broadcasted_iota(jnp.int32, (4 * lanes, lanes), 0)
    col = lax.broadcasted_iota(jnp.int32, (4 * lanes, lanes), 1)
    return jnp.where(lax.shift_right_logical(row, 2) == col, 1.0, 0.0).astype(bf16)


def same_low(lanes):
    row = lax.broadcasted_iota(jnp.int32, (4 * lanes, 4 * lanes), 0)
    col = lax.broadcasted_iota(jnp.int32, (4 * lanes, 4 * lanes), 1)
    return (row & 3) == (col & 3)


def widen(matrix):
    lanes = matrix.shape[0]
    spread = spread_matrix(lanes)
    keep = same_low(lanes)
    made = []
    for part in split(matrix):
        left = dot_of(spread, part, NN).astype(bf16)
        full = dot_of(left, spread, NT)
        made.append(jnp.where(keep, full, 0.0).astype(bf16))
    return tuple(made)


def quads(ref):
    count = ref.shape[0] // 4
    return jnp.concatenate([ref[pl.ds(q, count, stride=4), :] for q in range(4)], axis=1)


def apply_quads(dst, values, matrix):
    lanes = matrix.shape[0]
    result = dot3(values, widen(matrix))
    count = result.shape[0]
    for q in range(4):
        dst[pl.ds(q, count, stride=4), :] = result[:, q * lanes : (q + 1) * lanes]


def gram_quads(left, right):
    lanes = left[0].shape[1] // 4
    full = jnp.where(same_low(lanes), dot3(left, right, TN), 0.0)
    spread = spread_matrix(lanes)
    fh, fl = split(full)
    half = dot_of(fh, spread, NN) + dot_of(fl, spread, NN)
    hh, hl = split(half)
    return dot_of(spread, hh, TN) + dot_of(spread, hl, TN)


def mid_starts(rows, mid_count, lanes):
    stride = min(2 ** (YQ - 1), mid_count // lanes)
    groups = rows // (stride * lanes)
    return [g * stride * lanes + s for g in range(groups) for s in range(stride)], stride


def build_gates(pairs, cosines, sines, ut, u, which):
    lanes = ut.shape[1]
    givens = cosines.shape[1]
    lane = lax.broadcasted_iota(jnp.int32, (8, lanes), 1)
    row = lax.broadcasted_iota(jnp.int32, (lanes, lanes), 0)
    col = lax.broadcasted_iota(jnp.int32, (lanes, lanes), 1)
    for b in which:
        ut[b] = jnp.where(row == col, 1.0, 0.0)
    for g in range(givens):
        for b in which:
            p = pairs[b, 0, g]
            s = pairs[b, 1, g]
            low = lax.shift_right_logical(lane, p) & 1
            high = lax.shift_right_logical(lane, s) & 1
            cosine = jnp.broadcast_to(cosines[b : b + 1, g : g + 1], (8, lanes))
            sine = jnp.broadcast_to(sines[b : b + 1, g : g + 1], (8, lanes))
            keep = jnp.where(low != high, cosine, 1.0)[:1]
            up = jnp.where(low < high, -sine, 0.0)[:1]
            down = jnp.where(low > high, sine, 0.0)[:1]
            gap = lax.shift_left(jnp.int32(1), p) - lax.shift_left(jnp.int32(1), s)
            now = ut[b]
            ut[b] = (
                now * keep
                + pltpu.roll(now, (lanes - gap) & (lanes - 1), 1) * up
                + pltpu.roll(now, (lanes + gap) & (lanes - 1), 1) * down
            )
    for b in which:
        u[b] = jnp.transpose(ut[b])


def hop_matrix(size, terms):
    row = lax.broadcasted_iota(jnp.int32, (size, size), 0)
    col = lax.broadcasted_iota(jnp.int32, (size, size), 1)
    gap = row ^ col
    total = jnp.zeros((size, size), f32)
    for lower, upper, weight in terms:
        differ = (lax.shift_right_logical(row, lower) & 1) != (
            lax.shift_right_logical(row, upper) & 1
        )
        total = total + jnp.where(differ & (gap == (1 << lower | 1 << upper)), weight, 0.0)
    return total


def flip_matrix(size, bit, side, weight):
    row = lax.broadcasted_iota(jnp.int32, (size, size), 0)
    col = lax.broadcasted_iota(jnp.int32, (size, size), 1)
    active = ((lax.shift_right_logical(row, bit) & 1) != side) & ((row ^ col) == (1 << bit))
    return jnp.where(active, weight, 0.0)


def main_kernel(
    n, mid_count, ranks, pairs, coef, mask, angles, s0,
    adj, grads,
    ut, u, s1, s2, s3,
    xb, s4, yb, zb, rungs, chain, l4, l3, back, l2,
    part_a, part_b, lent_a, lent_b, got_a, got_b, sum_a, sum_b, full_a, full_b,
    sem_a, sem_x, sem_b, sem_r,
):
    me = lax.axis_index(AXIS)
    top_local, _, lanes = s3.shape
    top, low, _ = xb.shape
    rows = top * low
    low_bits = low.bit_length() - 1
    top_bits = top.bit_length() - 1
    lane_bits = lanes.bit_length() - 1
    flat = lambda ref: ref.reshape(rows, lanes)
    mid_flat = top_local * mid_count

    def each_peer(body):
        def step(d, carry):
            body(lax.rem(me + d, n))
            return carry
        lax.fori_loop(1, n, step, 0)

    barrier = pltpu.get_barrier_semaphore()
    each_peer(lambda peer: pl.semaphore_signal(barrier, inc=1, device_id={AXIS: peer}))

    cosines = jnp.cos(angles[...])
    sines = jnp.sin(angles[...])
    build_gates(pairs, cosines, sines, ut, u, (0, 1, 2))
    starts, stride = mid_starts(mid_flat, mid_count, lanes)
    apply_lanes(s1, s0, ut[0])
    apply_quads(s2, quads(s1), ut[1])
    apply_rows(s3.reshape(mid_flat, lanes), s2, u[2], starts, lanes, stride)
    pl.semaphore_wait(barrier, n - 1)

    def remote(src, dst, send, recv, peer):
        return pltpu.make_async_remote_copy(
            src_ref=src, dst_ref=dst, send_sem=send, recv_sem=recv, device_id={AXIS: peer}
        )

    def settle(ref, send, recv):
        whole = remote(ref, ref, send, recv, lax.rem(me + 1, n))
        whole.wait_recv()
        whole.wait_send()

    mine_rows = pl.ds(pl.multiple_of(me * top_local, top_local), top_local)
    mine_mid = pl.ds(pl.multiple_of(me * low, low), low)

    each_peer(
        lambda peer: remote(
            s3.at[:, pl.ds(pl.multiple_of(peer * low, low), low), :],
            xb.at[mine_rows], sem_a.at[0], sem_a.at[1], peer,
        ).start()
    )
    xb[mine_rows] = s3[:, mine_mid, :]

    build_gates(pairs, cosines, sines, ut, u, (3, 4))
    weights = [coef[h] * mask[h].astype(f32) for h in range(coef.shape[0])]
    first_top = lane_bits + YQ
    first_rung = first_top + top_bits - 1
    lane_hops = split(hop_matrix(lanes, [(h, h + 1, weights[h]) for h in range(lane_bits - 1)]))
    top_hops = split(
        hop_matrix(top, [(k, k + 1, weights[first_top + k]) for k in range(top_bits - 1)])
    )
    flips = [
        [split(flip_matrix(top, k, side, weights[first_rung + k])) for side in range(2)]
        for k in range(low_bits)
    ]

    settle(xb.at[pl.ds(0, (n - 1) * top_local)], sem_a.at[0], sem_a.at[1])

    xf, s4f, l4f, l3f = flat(xb), s4, l4, flat(l3)
    near = [a * lanes for a in range(rows // lanes)]
    planes = list(range(low))
    apply_rows(s4f, xf, u[3], near, lanes, 1)
    u4 = split(u[4])
    inner = yb.shape[1:]
    own_bits = [lax.rem(me // (2**k), 2) for k in range(ranks)]
    half_low = low // 2

    def half(ref, k, side):
        where = (slice(None),) * (ranks - 1 - k) + (side,)
        return ref.at[where]

    def partner(k):
        return me + (1 - 2 * own_bits[k]) * 2**k

    for c in planes:
        yb[c] = dot3(u4, s4f[pl.ds(c, top, stride=low), :]).reshape(inner)
        for k in range(ranks - 1, -1, -1):
            remote(
                half(yb.at[c], k, 1 - own_bits[k]), rungs.at[k, c],
                sem_x.at[0, k], sem_x.at[1, k], partner(k),
            ).start()
    remote(
        yb.at[pl.ds((1 - own_bits[0]) * half_low, half_low)], chain,
        sem_x.at[0, ranks], sem_x.at[1, ranks], partner(0),
    ).start()

    lane = lax.broadcasted_iota(jnp.int32, (top, lanes), 1)
    lane_top = lax.shift_right_logical(lane, lane_bits - 1) & 1
    values = lambda c: yb[c].reshape(top, lanes)
    for c in planes:
        own = split(values(c))
        total = dot3(own, lane_hops) + dot3(top_hops, own)
        for k in range(low_bits):
            total = total + dot3(flips[k][c >> k & 1], values(c ^ 1 << k))
        for k in range(low_bits - 1):
            if (c >> k & 1) != (c >> (k + 1) & 1):
                total = total + weights[lane_bits + k] * values(c ^ 3 << k)
        rolled = pltpu.roll(values(c ^ 1), lanes // 2, 1)
        total = total + jnp.where(lane_top != (c & 1), weights[lane_bits - 1] * rolled, 0.0)
        zb[c] = total.reshape(inner)

    seat = pl.ds((1 - own_bits[0]) * half_low, half_low)
    settle(chain, sem_x.at[0, ranks], sem_x.at[1, ranks])
    zb[seat] = zb[seat] + weights[lane_bits + low_bits - 1] * chain[...]
    for k in range(ranks):
        settle(rungs.at[k], sem_x.at[0, k], sem_x.at[1, k])
        for c in planes:
            place = half(zb.at[c], k, 1 - own_bits[k])
            place[...] = place[...] + weights[first_rung + low_bits + k] * rungs[k, c]

    ut4 = split(ut[4])
    for c in planes:
        l4f[pl.ds(c, top, stride=low), :] = dot3(ut4, zb[c].reshape(top, lanes))
    apply_rows(l3f, l4f, ut[3], near, lanes, 1)

    each_peer(
        lambda peer: remote(
            l3.at[pl.ds(pl.multiple_of(peer * top_local, top_local), top_local)],
            back.at[:, mine_mid, :], sem_b.at[0], sem_b.at[1], peer,
        ).start()
    )
    back[:, mine_mid, :] = l3[mine_rows]
    gram = None
    for c in range(0, low, 2):
        lam = jnp.concatenate([zb[c + i].reshape(top, lanes) for i in range(2)], axis=1)
        old = jnp.concatenate(
            [s4f[pl.ds(c + i, top, stride=low), :] for i in range(2)], axis=1
        )
        part = dot3(lam, old, NT)
        gram = part if gram is None else gram + part
    part_a[pl.ds(2 * lanes, lanes), :] = gram
    part_a[pl.ds(lanes, lanes), :] = gram_rows(l4f, xf, near, lanes, 1)

    factor = 2.0 / (top * mid_count)
    mate = partner(0)
    pairs_of = n // 2

    def each_twin(body):
        def step(d, carry):
            body(lax.rem(me + 2 * d, n))
            return carry
        lax.fori_loop(1, pairs_of, step, 0)

    def own_half(chunk, side):
        size = pairs_of * chunk
        return pl.ds(pl.multiple_of(side * size, 8), size)

    def lend(part, lent, chunk, number):
        remote(
            part.at[own_half(chunk, 1 - own_bits[0])], lent,
            sem_r.at[0, number], sem_r.at[1, number], mate,
        ).start()

    def scatter(part, lent, got, chunk, number):
        settle(lent, sem_r.at[0, number], sem_r.at[1, number])
        lent[...] = lent[...] + part[own_half(chunk, own_bits[0]), :]
        each_twin(
            lambda peer: remote(
                lent.at[pl.ds(pl.multiple_of(peer // 2 * chunk, 8), chunk)], got.at[me // 2],
                sem_r.at[0, number + 1], sem_r.at[1, number + 1], peer,
            ).start()
        )
        got[me // 2] = lent[pl.ds(pl.multiple_of(me // 2 * chunk, 8), chunk), :]

    def combine(got, mine, full, chunk, number):
        settle(got.at[pl.ds(0, pairs_of - 1)], sem_r.at[0, number + 1], sem_r.at[1, number + 1])
        mine[...] = factor * jnp.sum(got[...], axis=0)
        spot = pl.ds(
            pl.multiple_of(own_bits[0] * pairs_of * chunk + me // 2 * chunk, 8), chunk
        )
        each_twin(
            lambda peer: remote(
                mine, full.at[spot], sem_r.at[0, number + 2], sem_r.at[1, number + 2], peer
            ).start()
        )
        full[spot, :] = mine[...]

    def trade(full, chunk, number):
        settle(
            full.at[pl.ds(0, (pairs_of - 1) * chunk)],
            sem_r.at[0, number + 2], sem_r.at[1, number + 2],
        )
        whole = full.at[own_half(chunk, own_bits[0])]
        remote(whole, whole, sem_r.at[0, number + 3], sem_r.at[1, number + 3], mate).start()

    def finish(full, chunk, number):
        settle(
            full.at[pl.ds(0, pairs_of * chunk)],
            sem_r.at[0, number + 3], sem_r.at[1, number + 3],
        )

    chunk_a = sum_a.shape[0]
    chunk_b = sum_b.shape[0]
    for part, chunk, count in ((part_a, chunk_a, 3), (part_b, chunk_b, 2)):
        spare = n * chunk - count * lanes
        if spare > 0:
            part[pl.ds(count * lanes, spare), :] = jnp.zeros((spare, lanes), f32)
    low_part = pl.ds(0, (n - 1) * low)
    settle(back.at[:, low_part, :], sem_b.at[0], sem_b.at[1])
    backf = back.reshape(mid_flat, lanes)
    part_a[pl.ds(0, lanes), :] = gram_rows(backf, s2, starts, lanes, stride)
    lend(part_a, lent_a, chunk_a, 0)
    apply_rows(l2, backf, ut[2], starts, lanes, stride)
    wide = split(quads(l2))
    apply_quads(l2, wide, u[1])
    scatter(part_a, lent_a, got_a, chunk_a, 0)
    part_b[pl.ds(lanes, lanes), :] = gram_quads(wide, split(quads(s1)))
    part_b[pl.ds(0, lanes), :] = gram_lanes(l2, s0)
    lend(part_b, lent_b, chunk_b, 4)
    scatter(part_b, lent_b, got_b, chunk_b, 4)
    combine(got_a, sum_a, full_a, chunk_a, 0)
    apply_lanes(adj, l2, u[0])
    combine(got_b, sum_b, full_b, chunk_b, 4)
    trade(full_a, chunk_a, 0)
    trade(full_b, chunk_b, 4)
    finish(full_a, chunk_a, 0)
    grads[pl.ds(2 * lanes, 3 * lanes), :] = full_a[pl.ds(0, 3 * lanes), :]
    finish(full_b, chunk_b, 4)
    grads[pl.ds(0, 2 * lanes), :] = full_b[pl.ds(0, 2 * lanes), :]


def on_device(initial_state, gate_angles, gate_pairs, hop_coef, hop_mask):
    top_local, mid_count, lanes = initial_state.shape
    blocks = gate_angles.shape[0]
    n = lax.axis_size(AXIS)
    top = top_local * n
    low = mid_count // n
    rows = top_local * mid_count
    ranks = (top // low).bit_length() - 1
    vmem = pl.BlockSpec(memory_space=pltpu.VMEM)
    smem = pl.BlockSpec(memory_space=pltpu.SMEM)
    flat = jax.ShapeDtypeStruct((rows, lanes), f32)
    gates = (blocks, lanes, lanes)
    s0 = initial_state.reshape(rows, lanes)
    chunk_a = 8 * -(-3 * lanes // (8 * n))
    chunk_b = 8 * -(-2 * lanes // (8 * n))
    bits = (low,) + (2,) * ranks + (top >> ranks, lanes)
    half = (ranks, low) + (2,) * (ranks - 1) + (top >> ranks, lanes)
    full = (rows, lanes)
    tall = (top, low, lanes)
    adjoint, grads = pl.pallas_call(
        functools.partial(main_kernel, n, mid_count, ranks),
        out_shape=[flat, jax.ShapeDtypeStruct((blocks * lanes, lanes), f32)],
        in_specs=[smem] * 3 + [vmem] * 2,
        out_specs=[vmem] * 2,
        scratch_shapes=[
            pltpu.VMEM(gates, f32),
            pltpu.VMEM(gates, f32),
            pltpu.VMEM(full, f32),
            pltpu.VMEM(full, f32),
            pltpu.VMEM(initial_state.shape, f32),
            pltpu.VMEM(tall, f32),
            pltpu.VMEM(full, f32),
            pltpu.VMEM(bits, f32),
            pltpu.VMEM(bits, f32),
            pltpu.VMEM(half, f32),
            pltpu.VMEM((low // 2,) + bits[1:], f32),
            pltpu.VMEM(full, f32),
            pltpu.VMEM(tall, f32),
            pltpu.VMEM(initial_state.shape, f32),
            pltpu.VMEM(full, f32),
            pltpu.VMEM((n * chunk_a, lanes), f32),
            pltpu.VMEM((n * chunk_b, lanes), f32),
            pltpu.VMEM((n // 2 * chunk_a, lanes), f32),
            pltpu.VMEM((n // 2 * chunk_b, lanes), f32),
            pltpu.VMEM((n // 2, chunk_a, lanes), f32),
            pltpu.VMEM((n // 2, chunk_b, lanes), f32),
            pltpu.VMEM((chunk_a, lanes), f32),
            pltpu.VMEM((chunk_b, lanes), f32),
            pltpu.VMEM((n * chunk_a, lanes), f32),
            pltpu.VMEM((n * chunk_b, lanes), f32),
            pltpu.SemaphoreType.DMA((2,)),
            pltpu.SemaphoreType.DMA((2, ranks + 1)),
            pltpu.SemaphoreType.DMA((2,)),
            pltpu.SemaphoreType.DMA((2, 8)),
        ],
        compiler_params=pltpu.CompilerParams(collective_id=0, has_side_effects=True),
        name="main",
    )(jnp.transpose(gate_pairs, (0, 2, 1)), hop_coef, hop_mask, gate_angles, s0)
    return adjoint.reshape(initial_state.shape), grads.reshape(blocks, lanes, lanes)


def solution(mesh):
    in_specs = (P(("runs", AXIS), None, None), P("runs", None), P(), P(), P())
    out_specs = (P(("runs", AXIS), None, None), P("runs", None, None))
    return jax.shard_map(
        on_device, mesh=mesh, in_specs=in_specs, out_specs=out_specs, check_vma=False
    )
```
